32 devices in a mesh: srv: 2 (over y), blk: 8 (over z, x), rep: 2 (over core).
Axes of the slice: x: 2, y: 2, z: 4, core: 2. Of those that a mesh axis runs over, the one named last changes fastest.
Arguments:
- queries: bfloat16 [2, 8, 32, 4096], P('srv', 'blk', 'rep'), parts along dimension 2, may hold values from -16 to 16
- destination: int32 [2, 8, 8], P('srv', 'blk', 'rep'), parts along dimension 2, may hold values from 0 to 1, as said below
- offsets: int32 [2, 8, 8], P('srv', 'blk', 'rep'), parts along dimension 2, may hold values from 0 to 124
- key_rows: bfloat16 [2, 1024, 512], P('srv', 'blk', 'rep'), parts along dimension 2, may hold values from -16 to 16
- value_rows: bfloat16 [2, 1024, 512], P('srv', 'blk', 'rep'), parts along dimension 2, may hold values from -6 to 6
- lengths: int32 [2, 16], P('srv', 'rep'), parts along dimension 1, may hold values from 1 to 385, 1024 in all within a row
Outputs:
- attended: bfloat16 [2, 8, 32, 4096], P('srv', 'blk', 'rep'), parts along dimension 2
The draws below stay inside these ranges and needn't reach their ends.
There are 2 independent parts, one for each index of `rep`. The reference program is written for one: setup_inputs(seed, part) draws one part's arguments, and reference() takes and returns one part's arrays. A program takes and returns all parts, laid end to end along the dimension named above; each array names one. Nothing has to cross between parts.
Inputs may be any that keep to these rules, and one draw needn't show every extreme that they name: `destination`: within each round (tasks r * 2 to r * 2 + 1 of a device) a device names 2 different servers; in each round and for each blk index, 2 servers are named by every device of that blk index.
All inputs are finite; a program needn't handle non-finite values.
Results may differ from the reference program's by a relative error of at most 0.0033.
Values may be sent and summed in bfloat16 or wider, within the bound.
A program may use at most 64 MiB of HBM per device.

```python
import math
import jax
import jax.numpy as jnp
import numpy as np
from jax import lax

QH = 32
KVH = 2
HD = 128
KVB = 128
R = 4
ROUNDS = 2
HOT = 2
DOCS = 8
TASKS = 2
CTX = 1024
N_SRV = 2
N_BLK = 8


def server_order(subkey):
    return jax.random.permutation(subkey, N_SRV)


def task_order(subkey):
    return jax.random.permutation(subkey, TASKS)


def draw_queries(key, part):
    shape = (N_SRV, N_BLK, ROUNDS * TASKS * R, QH * HD)
    base = jnp.clip(jax.random.normal(jax.random.fold_in(key, 11), shape, jnp.float32), -6.0, 6.0)
    return base.astype(jnp.bfloat16)


def draw_key_rows(key, part):
    shape = (N_SRV, CTX, KVH * HD)
    base = jnp.clip(jax.random.normal(jax.random.fold_in(key, 31), shape, jnp.float32), -6.0, 6.0)
    return base.astype(jnp.bfloat16)


def draw_destination(key, part):
    hot_keys = jax.random.split(jax.random.fold_in(key, 21), N_BLK * ROUNDS)
    hot_list = jax.vmap(server_order)(hot_keys)[:, :HOT]
    everyone = jnp.arange(N_SRV, dtype=jnp.int32)
    is_hot = jnp.any(hot_list[:, :, None] == everyone[None, None, :], axis=1).astype(jnp.int32)
    is_hot = is_hot.reshape(N_BLK, ROUNDS, N_SRV)
    rank_keys = jax.random.split(jax.random.fold_in(key, 22), N_SRV * N_BLK * ROUNDS)
    ranks = jax.vmap(server_order)(rank_keys).reshape(N_SRV, N_BLK, ROUNDS, N_SRV).astype(jnp.int32)
    scores = ranks + N_SRV * is_hot[None]
    picked = lax.top_k(scores, TASKS)[1]
    shuffle_keys = jax.random.split(jax.random.fold_in(key, 23), N_SRV * N_BLK * ROUNDS)
    shuffle = jax.vmap(task_order)(shuffle_keys).reshape(N_SRV, N_BLK, ROUNDS, TASKS)
    picked = jnp.take_along_axis(picked, shuffle, axis=3)
    return picked.reshape(N_SRV, N_BLK, ROUNDS * TASKS).astype(jnp.int32)


def touch_ends(values, stream_key, low, largest):
    place = [jax.random.randint(jax.random.fold_in(stream_key, axis), (), 0, length) for axis, length in enumerate(values.shape)]
    widest = values.shape.index(max(values.shape))
    beside = place[:widest] + [(place[widest] + 1) % values.shape[widest]] + place[widest + 1:]
    return values.at[tuple(place)].set(low).at[tuple(beside)].set(largest)


def levels(stream_key, extent, pieces, smallest, top_value):
    loudness = 1.0
    for dim, shards_of in pieces:
        heights = jax.random.uniform(jax.random.fold_in(jax.random.fold_in(stream_key, 6), dim), (shards_of,), jnp.float32, smallest / len(pieces), top_value / len(pieces))
        loudness = loudness * jnp.repeat(jnp.exp(heights), extent[dim] // shards_of).reshape((-1,) + (1,) * (len(extent) - 1 - dim))
    return loudness


def split_up(amount, total, most, slope):
    portions = [(1 << 20) // math.isqrt(grade ** slope) + 1 for grade in range(2, amount + 1)]
    surplus, holding = total - most - (amount - 1), [1] * (amount - 1)
    while surplus > 0:
        candidates = [i for i in range(amount - 1) if holding[i] < most]
        pool, budget = sum([portions[i] for i in candidates]), surplus
        for i in candidates:
            addition = min(most - holding[i], max(1, budget * portions[i] // pool), surplus)
            holding[i] = holding[i] + addition
            surplus = surplus - addition
    return np.array([most] + holding)


def ragged_sizes(stream_key, count, total, most, lean):
    if count == 2:
        one = jax.random.randint(stream_key, (), max(1, total - most), min(most, total - 1) + 1)
        return jnp.stack([one, total - one])
    sizes = jnp.asarray(split_up(count, total, most, lean), jnp.int32)
    twos = (count - 1) // 2
    source_of, taker = sizes[1:1 + 2 * twos:2], sizes[2:2 + 2 * twos:2]
    slack = jnp.minimum(source_of - 1, most - taker)
    passed = jax.random.randint(jax.random.fold_in(stream_key, 1), (twos,), 0, 1 << 20) % (slack + 1)
    sizes = sizes.at[1:1 + 2 * twos:2].set(source_of - passed).at[2:2 + 2 * twos:2].set(taker + passed)
    return sizes[jax.random.permutation(jax.random.fold_in(stream_key, 2), count)]


def centred(key, extent, scale, most, shards=(), kind=jnp.bfloat16):
    gain = levels(key, extent, shards, -0.22, 0.18) if shards else 1.0
    entries = jax.random.normal(key, extent, jnp.float32) * scale * gain
    return jnp.minimum(jnp.maximum(entries, -most), most).astype(kind)


def setup_inputs(seed: int = 0, part: int = 0) -> dict:
    seeds = jax.random.split(jax.random.key(seed), 7)
    part_splits = jax.random.split(jax.random.fold_in(seeds[6], part), 7)
    queries = draw_queries(jax.random.fold_in(jax.random.fold_in(seeds[6], part), 71), part)
    destination = draw_destination(jax.random.fold_in(jax.random.fold_in(seeds[6], part), 71), part)
    offsets = touch_ends(jax.random.randint(part_splits[2], (N_SRV, N_BLK, ROUNDS * TASKS), 0, KVB - R + 1), jax.random.fold_in(part_splits[2], 1), 0, KVB - R).astype(jnp.int32)
    key_rows = draw_key_rows(jax.random.fold_in(jax.random.fold_in(seeds[6], part), 71), part)
    value_rows = centred(part_splits[4], (N_SRV, CTX, KVH * HD), 1.0, 6.0, ((0, 2), (1, 8)))
    lengths = jax.vmap(lambda own: ragged_sizes(own, DOCS, CTX, 3 * KVB + 1, 1))(jax.random.split(part_splits[5], N_SRV)).reshape((N_SRV, DOCS)).astype(jnp.int32)
    return dict(queries=queries, destination=destination, offsets=offsets, key_rows=key_rows, value_rows=value_rows, lengths=lengths)


def attend_task(query_block, target, start, column, key_rows, value_rows, boundary):
    span = 3 * KVB + R
    groups = QH // KVH
    scaling = 1.0 / math.sqrt(HD)
    target = target.astype(jnp.int32)
    first = (column * KVB + start).astype(jnp.int32)
    anchor = jnp.clip(first - 3 * KVB, 0, CTX - span).astype(jnp.int32)
    zero = jnp.zeros((), jnp.int32)
    key_block = lax.dynamic_slice(key_rows, (target, anchor, zero), (1, span, KVH * HD))[0]
    value_block = lax.dynamic_slice(value_rows, (target, anchor, zero), (1, span, KVH * HD))[0]
    ends = lax.dynamic_slice(boundary, (target, zero), (1, DOCS))[0]
    query_pos = first + jnp.arange(R, dtype=jnp.int32)
    key_pos = anchor + jnp.arange(span, dtype=jnp.int32)
    query_doc = lax.optimization_barrier(jnp.sum((ends[None, :] <= query_pos[:, None]).astype(jnp.int32), axis=1))
    key_doc = lax.optimization_barrier(jnp.sum((ends[None, :] <= key_pos[:, None]).astype(jnp.int32), axis=1))
    allowed = (key_pos[None, :] <= query_pos[:, None]) & (key_doc[None, :] == query_doc[:, None])
    query_heads = query_block.astype(jnp.float32).reshape(R, KVH, groups, HD)
    key_heads = key_block.astype(jnp.float32).reshape(span, KVH, HD)
    value_heads = value_block.astype(jnp.float32).reshape(span, KVH, HD)
    scores = jnp.einsum('rkgd,nkd->kgrn', query_heads, key_heads) * scaling
    scores = jnp.where(allowed[None, None], scores, -1e+30)
    highest = lax.optimization_barrier(jnp.max(scores, axis=3, keepdims=True))
    weights = jnp.exp(scores - highest)
    denominator = lax.optimization_barrier(jnp.sum(weights, axis=3))
    rounded = lax.optimization_barrier(weights.astype(jnp.bfloat16)).astype(jnp.float32)
    weighted = jnp.einsum('kgrn,nkd->rkgd', rounded, value_heads)
    result = weighted / jnp.transpose(denominator, (2, 0, 1))[..., None]
    return result.reshape(R, QH * HD).astype(jnp.bfloat16)

def reference(queries, destination, offsets, key_rows, value_rows, lengths):
    boundary = jnp.cumsum(lengths, axis=1).astype(jnp.int32)
    task_count = ROUNDS * TASKS
    flat_queries = queries.reshape(N_SRV * N_BLK, task_count, R, QH * HD)
    flat_targets = destination.reshape(N_SRV * N_BLK, task_count)
    flat_starts = offsets.reshape(N_SRV * N_BLK, task_count)
    columns = jnp.tile(jnp.arange(N_BLK, dtype=jnp.int32), N_SRV)

    def one_device(bundle):
        query_group, target_group, start_group, column = bundle

        def per_task(query_block, target, start):
            return attend_task(query_block, target, start, column, key_rows, value_rows, boundary)
        return jax.vmap(per_task)(query_group, target_group, start_group)
    answers = lax.map(one_device, (flat_queries, flat_targets, flat_starts, columns))
    return answers.reshape(N_SRV, N_BLK, task_count * R, QH * HD)
```

```python
import math

import jax
import jax.numpy as jnp
from jax import lax
from jax.experimental import pallas as pl
from jax.experimental.pallas import tpu as pltpu
from jax.sharding import PartitionSpec as P

QH = 32
KVH = 2
HD = 128
R = 4
ROUNDS = 2
BACK = 3
LANES = 128
MESH = pl.DeviceIdType.MESH


def each(count, body):
    if count <= 2:
        for index in range(count):
            body(index)
    else:
        lax.fori_loop(0, count, lambda index, carry: (body(index), carry)[1], 0)


def kernel(
    servers,
    blocks,
    destination,
    offsets,
    lengths,
    queries,
    key_rows,
    value_rows,
    out,
    own_queries,
    keys,
    values,
    query_out,
    query_in,
    place_out,
    place_in,
    scores,
    answers,
    returned,
    load_sem,
    kv_send,
    kv_recv,
    query_send,
    query_recv,
    place_send,
    place_recv,
    back_send,
    back_recv,
):
    me = lax.axis_index("srv")
    blk = lax.axis_index("blk")
    block_rows = key_rows.shape[1]
    tasks = destination.shape[2]
    per_round = tasks // ROUNDS
    groups = QH // KVH
    slot_rows = ROUNDS * R
    head_rows = groups * slot_rows
    scaling = 1.0 / math.sqrt(HD)
    docs = lengths.shape[1]

    load_queries = pltpu.make_async_copy(queries.at[0, 0], own_queries, load_sem.at[0])
    load_keys = pltpu.make_async_copy(
        key_rows.at[0], keys.at[pl.ds(0, block_rows)], load_sem.at[1]
    )
    load_values = pltpu.make_async_copy(
        value_rows.at[0], values.at[pl.ds(0, block_rows)], load_sem.at[2]
    )
    load_queries.start()
    load_keys.start()
    load_values.start()

    barrier = pltpu.get_barrier_semaphore()
    for hop in range(1, BACK + 1):

        @pl.when(blk + hop < blocks)
        def _():
            pl.semaphore_signal(
                barrier, inc=1, device_id={"blk": blk + hop}, device_id_type=MESH
            )

        @pl.when(blk >= hop)
        def _():
            pl.semaphore_signal(
                barrier, inc=1, device_id={"blk": blk - hop}, device_id_type=MESH
            )

    def greet(step):
        peer = lax.rem(me + 1 + step, servers)
        pl.semaphore_signal(barrier, inc=1, device_id={"srv": peer}, device_id_type=MESH)

    each(servers - 1, greet)

    for hop in range(1, BACK + 1):

        @pl.when(blk < hop)
        def _():
            empty = jnp.zeros((block_rows, keys.shape[1]), keys.dtype)
            keys[pl.ds(hop * block_rows, block_rows), :] = empty
            values[pl.ds(hop * block_rows, block_rows), :] = empty

    load_queries.wait()
    all_rows = own_queries[...]
    row = lax.broadcasted_iota(jnp.int32, (slot_rows, tasks * R), 0)
    column = lax.broadcasted_iota(jnp.int32, (slot_rows, tasks * R), 1)
    column_target = jnp.full((slot_rows, tasks * R), -1, jnp.int32)
    for task in range(tasks):
        column_target = jnp.where(
            column // R == task, destination[0, 0, task], column_target
        )
    same_place = (row // R == column // (per_round * R)) & (row % R == column % R)
    place_row = lax.broadcasted_iota(jnp.int32, (slot_rows, LANES), 0)

    def pack(slot):
        chosen = jnp.where(same_place & (column_target == slot), 1.0, 0.0).astype(jnp.bfloat16)
        routed = jnp.dot(chosen, all_rows, preferred_element_type=jnp.float32)
        for g in range(KVH):
            parts = [
                routed[:, (g * groups + h) * HD : (g * groups + h + 1) * HD]
                for h in range(groups)
            ]
            query_out[slot, g] = jnp.concatenate(parts, axis=0).astype(jnp.bfloat16)
        start = jnp.zeros((slot_rows, LANES), jnp.int32)
        for turn in range(ROUNDS):
            offset = jnp.int32(0)
            for t in range(per_round):
                task = turn * per_round + t
                offset = jnp.where(
                    destination[0, 0, task] == slot, offsets[0, 0, task], offset
                )
            start = jnp.where(place_row // R == turn, offset, start)
        place_out[slot] = start + place_row % R + blk * block_rows

    each(servers, pack)

    neighbours = (
        jnp.minimum(blk, BACK) + jnp.minimum(blocks - 1 - blk, BACK) + (servers - 1)
    )
    pl.semaphore_wait(barrier, neighbours)

    def query_copy(slot, source):
        return pltpu.make_async_remote_copy(
            src_ref=query_out.at[slot],
            dst_ref=query_in.at[source],
            send_sem=query_send.at[slot],
            recv_sem=query_recv.at[source],
            device_id={"srv": slot},
            device_id_type=MESH,
        )

    def place_copy(slot, source):
        return pltpu.make_async_remote_copy(
            src_ref=place_out.at[slot],
            dst_ref=place_in.at[source],
            send_sem=place_send.at[slot],
            recv_sem=place_recv.at[source],
            device_id={"srv": slot},
            device_id_type=MESH,
        )

    def back_copy(slot, g, server):
        return pltpu.make_async_remote_copy(
            src_ref=answers.at[slot, g],
            dst_ref=returned.at[server, g],
            send_sem=back_send.at[slot, g],
            recv_sem=back_recv.at[server, g],
            device_id={"srv": slot},
            device_id_type=MESH,
        )

    def kv_copy(hop, which):
        source, target = ((key_rows, keys), (value_rows, values))[which]
        return pltpu.make_async_remote_copy(
            src_ref=source.at[0],
            dst_ref=target.at[pl.ds(hop * block_rows, block_rows)],
            send_sem=kv_send.at[hop - 1, which],
            recv_sem=kv_recv.at[hop - 1, which],
            device_id={"blk": blk + hop},
            device_id_type=MESH,
        )

    def send_queries(step):
        peer = lax.rem(me + 1 + step, servers)
        query_copy(peer, me).start()
        place_copy(peer, me).start()

    each(servers - 1, send_queries)
    for which in range(2):
        for hop in range(BACK, 0, -1):

            @pl.when(blk + hop < blocks)
            def _():
                kv_copy(hop, which).start()

    query_in[me] = query_out[me]
    place_in[me] = place_out[me]
    load_keys.wait()

    def score(slot, hop):
        for g in range(KVH):
            block = keys[pl.ds(hop * block_rows, block_rows), g * HD : (g + 1) * HD]
            scores[slot, g, :, hop * block_rows : (hop + 1) * block_rows] = lax.dot_general(
                query_in[slot, g],
                block,
                (((1,), (1,)), ((), ())),
                preferred_element_type=jnp.float32,
            )

    score(me, 0)

    def first_scores(step):
        peer = lax.rem(me + 1 + step, servers)
        query_copy(peer, peer).wait_recv()
        place_copy(peer, peer).wait_recv()
        score(peer, 0)

    each(servers - 1, first_scores)
    for hop in range(1, BACK + 1):

        @pl.when(blk >= hop)
        def _():
            kv_copy(hop, 0).wait_recv()

        each(servers, lambda slot: score(slot, hop))
    load_values.wait()
    for hop in range(1, BACK + 1):

        @pl.when(blk >= hop)
        def _():
            kv_copy(hop, 1).wait_recv()

    ends = []
    running = jnp.int32(0)
    for doc in range(docs):
        running = running + lengths[0, doc]
        ends.append(running)
    lane = lax.broadcasted_iota(jnp.int32, (slot_rows, LANES), 1)

    def attend(slot, g):
        place = place_in[slot]
        first = jnp.zeros_like(place)
        for end in ends:
            first = jnp.where(end <= place, end, first)
        pieces = []
        highest = None
        for hop in range(BACK + 1):
            for part in range(block_rows // LANES):
                low = hop * block_rows + part * LANES
                at = (blk - hop) * block_rows + part * LANES + lane
                allowed = (at <= place) & (at >= first)
                piece = scores[slot, g, :, low : low + LANES] * scaling
                piece = piece.reshape(groups, slot_rows, LANES)
                piece = jnp.where(allowed[None], piece, -1e30)
                pieces.append(piece)
                highest = piece if highest is None else jnp.maximum(highest, piece)
        highest = jnp.max(highest, axis=2, keepdims=True)
        weights = [jnp.exp(piece - highest) for piece in pieces]
        total = weights[0]
        for weight in weights[1:]:
            total = total + weight
        total = jnp.sum(total, axis=2, keepdims=True)
        joined = jnp.concatenate(
            [w.reshape(head_rows, LANES).astype(jnp.bfloat16) for w in weights], axis=1
        )
        weighted = jnp.dot(
            joined, values[:, g * HD : (g + 1) * HD], preferred_element_type=jnp.float32
        )
        return (weighted / total.reshape(head_rows, 1)).astype(jnp.bfloat16)

    def serve(step):
        peer = lax.rem(me + 1 + step, servers)
        for g in range(KVH):
            answers[peer, g] = attend(peer, g)
            back_copy(peer, g, me).start()

    each(servers - 1, serve)
    for g in range(KVH):
        returned[me, g] = attend(me, g)

    def collect(step):
        peer = lax.rem(me + 1 + step, servers)
        for g in range(KVH):
            back_copy(peer, g, peer).wait_recv()

    each(servers - 1, collect)

    out_row = lax.broadcasted_iota(jnp.int32, (tasks * R, servers * slot_rows), 0)
    from_row = lax.broadcasted_iota(jnp.int32, (tasks * R, servers * slot_rows), 1)
    row_target = jnp.full((tasks * R, servers * slot_rows), -1, jnp.int32)
    for task in range(tasks):
        row_target = jnp.where(out_row // R == task, destination[0, 0, task], row_target)
    within = from_row % slot_rows
    taken = (
        (row_target == from_row // slot_rows)
        & (within // R == out_row // (per_round * R))
        & (within % R == out_row % R)
    )
    taken = jnp.where(taken, 1.0, 0.0).astype(jnp.bfloat16)
    for g in range(KVH):
        got = [returned[slot, g].astype(jnp.float32) for slot in range(servers)]
        wide = []
        for h in range(groups):
            stacked = [piece[h * slot_rows : (h + 1) * slot_rows] for piece in got]
            wide.append(jnp.concatenate(stacked, axis=0).astype(jnp.bfloat16))
        wide = jnp.concatenate(wide, axis=1)
        out[0, 0, :, g * groups * HD : (g + 1) * groups * HD] = jnp.dot(
            taken, wide, preferred_element_type=jnp.float32
        ).astype(jnp.bfloat16)

    def finish(step):
        peer = lax.rem(me + 1 + step, servers)
        query_copy(peer, me).wait_send()
        place_copy(peer, me).wait_send()
        for g in range(KVH):
            back_copy(peer, g, me).wait_send()

    each(servers - 1, finish)
    for which in range(2):
        for hop in range(1, BACK + 1):

            @pl.when(blk + hop < blocks)
            def _():
                kv_copy(hop, which).wait_send()


def solution(mesh):
    servers = mesh.shape["srv"]
    blocks = mesh.shape["blk"]
    placed = (
        P("srv", "blk", "rep", None),
        P("srv", "blk", "rep"),
        P("srv", "blk", "rep"),
        P("srv", "blk", "rep"),
        P("srv", "blk", "rep"),
        P("srv", "rep"),
    )

    def on_device(queries, destination, offsets, key_rows, value_rows, lengths):
        block_rows, kv_width = key_rows.shape[1:]
        slot_rows = ROUNDS * R
        packed = (servers, KVH, QH // KVH * slot_rows, HD)
        window = (BACK + 1) * block_rows
        smem = pl.BlockSpec(memory_space=pltpu.SMEM)
        anywhere = pl.BlockSpec(memory_space=pl.ANY)
        dma = pltpu.SemaphoreType.DMA

        def body(*refs):
            kernel(servers, blocks, *refs)

        return pl.pallas_call(
            body,
            name="routed_attention",
            out_shape=jax.ShapeDtypeStruct(queries.shape, queries.dtype),
            in_specs=[smem] * 3 + [anywhere] * 3,
            out_specs=pl.BlockSpec(memory_space=pltpu.VMEM),
            scratch_shapes=[
                pltpu.VMEM(queries.shape[2:], jnp.bfloat16),
                pltpu.VMEM((window, kv_width), jnp.bfloat16),
                pltpu.VMEM((window, kv_width), jnp.bfloat16),
                pltpu.VMEM(packed, jnp.bfloat16),
                pltpu.VMEM(packed, jnp.bfloat16),
                pltpu.VMEM((servers, slot_rows, LANES), jnp.int32),
                pltpu.VMEM((servers, slot_rows, LANES), jnp.int32),
                pltpu.VMEM(packed[:3] + (window,), jnp.float32),
                pltpu.VMEM(packed, jnp.bfloat16),
                pltpu.VMEM(packed, jnp.bfloat16),
                dma((3,)),
                dma((BACK, 2)),
                dma((BACK, 2)),
                dma((servers,)),
                dma((servers,)),
                dma((servers,)),
                dma((servers,)),
                dma((servers, KVH)),
                dma((servers, KVH)),
            ],
            compiler_params=pltpu.CompilerParams(collective_id=0, has_side_effects=True),
        )(destination, offsets, lengths, queries, key_rows, value_rows)

    return jax.shard_map(
        on_device,
        mesh=mesh,
        in_specs=placed,
        out_specs=P("srv", "blk", "rep", None),
        check_vma=False,
    )
```

```python
import math

import jax
import jax.numpy as jnp
from jax import lax
from jax.experimental import pallas as pl
from jax.experimental.pallas import tpu as pltpu
from jax.sharding import PartitionSpec as P

QH = 32
KVH = 2
HD = 128
R = 4
ROUNDS = 2
BACK = 3
CHUNKS = 4
LANES = 128
MESH = pl.DeviceIdType.MESH


def each(count, body):
    if count <= 2:
        for index in range(count):
            body(index)
    else:
        lax.fori_loop(0, count, lambda index, carry: (body(index), carry)[1], 0)


def kernel(
    servers,
    blocks,
    destination,
    offsets,
    lengths,
    queries,
    key_rows,
    value_rows,
    out,
    own_queries,
    keys,
    values,
    query_out,
    query_in,
    place_out,
    place_in,
    scores,
    answers,
    returned,
    load_sem,
    own_send,
    relay_send,
    kv_recv,
    query_send,
    query_recv,
    place_send,
    place_recv,
    back_send,
    back_recv,
):
    me = lax.axis_index("srv")
    blk = lax.axis_index("blk")
    block_rows = key_rows.shape[1]
    tasks = destination.shape[2]
    per_round = tasks // ROUNDS
    groups = QH // KVH
    slot_rows = ROUNDS * R
    head_rows = groups * slot_rows
    scaling = 1.0 / math.sqrt(HD)
    docs = lengths.shape[1]

    load_queries = pltpu.make_async_copy(queries.at[0, 0], own_queries, load_sem.at[0])
    load_keys = pltpu.make_async_copy(
        key_rows.at[0], keys.at[pl.ds(0, block_rows)], load_sem.at[1]
    )
    load_values = pltpu.make_async_copy(
        value_rows.at[0], values.at[pl.ds(0, block_rows)], load_sem.at[2]
    )
    load_queries.start()
    load_keys.start()
    load_values.start()

    barrier = pltpu.get_barrier_semaphore()
    for hop in range(1, BACK):

        @pl.when(blk + hop < blocks)
        def _():
            pl.semaphore_signal(
                barrier, inc=1, device_id={"blk": blk + hop}, device_id_type=MESH
            )

        @pl.when(blk >= hop)
        def _():
            pl.semaphore_signal(
                barrier, inc=1, device_id={"blk": blk - hop}, device_id_type=MESH
            )

    def greet(step):
        peer = lax.rem(me + 1 + step, servers)
        pl.semaphore_signal(barrier, inc=1, device_id={"srv": peer}, device_id_type=MESH)

    each(servers - 1, greet)

    for hop in range(1, BACK + 1):

        @pl.when(blk < hop)
        def _():
            empty = jnp.zeros((block_rows, keys.shape[1]), keys.dtype)
            keys[pl.ds(hop * block_rows, block_rows), :] = empty
            values[pl.ds(hop * block_rows, block_rows), :] = empty

    load_queries.wait()
    all_rows = own_queries[...]
    row = lax.broadcasted_iota(jnp.int32, (slot_rows, tasks * R), 0)
    column = lax.broadcasted_iota(jnp.int32, (slot_rows, tasks * R), 1)
    column_target = jnp.full((slot_rows, tasks * R), -1, jnp.int32)
    for task in range(tasks):
        column_target = jnp.where(
            column // R == task, destination[0, 0, task], column_target
        )
    same_place = (row // R == column // (per_round * R)) & (row % R == column % R)
    place_row = lax.broadcasted_iota(jnp.int32, (slot_rows, LANES), 0)

    def pack(slot):
        chosen = jnp.where(same_place & (column_target == slot), 1.0, 0.0).astype(jnp.bfloat16)
        routed = jnp.dot(chosen, all_rows, preferred_element_type=jnp.float32)
        for g in range(KVH):
            parts = [
                routed[:, (g * groups + h) * HD : (g * groups + h + 1) * HD]
                for h in range(groups)
            ]
            query_out[slot, g] = jnp.concatenate(parts, axis=0).astype(jnp.bfloat16)
        start = jnp.zeros((slot_rows, LANES), jnp.int32)
        for turn in range(ROUNDS):
            offset = jnp.int32(0)
            for t in range(per_round):
                task = turn * per_round + t
                offset = jnp.where(
                    destination[0, 0, task] == slot, offsets[0, 0, task], offset
                )
            start = jnp.where(place_row // R == turn, offset, start)
        place_out[slot] = start + place_row % R + blk * block_rows

    each(servers, pack)

    neighbours = (
        jnp.minimum(blk, BACK - 1)
        + jnp.minimum(blocks - 1 - blk, BACK - 1)
        + (servers - 1)
    )
    pl.semaphore_wait(barrier, neighbours)

    def query_copy(slot, source):
        return pltpu.make_async_remote_copy(
            src_ref=query_out.at[slot],
            dst_ref=query_in.at[source],
            send_sem=query_send.at[slot],
            recv_sem=query_recv.at[source],
            device_id={"srv": slot},
            device_id_type=MESH,
        )

    def place_copy(slot, source):
        return pltpu.make_async_remote_copy(
            src_ref=place_out.at[slot],
            dst_ref=place_in.at[source],
            send_sem=place_send.at[slot],
            recv_sem=place_recv.at[source],
            device_id={"srv": slot},
            device_id_type=MESH,
        )

    def back_copy(slot, g, server):
        return pltpu.make_async_remote_copy(
            src_ref=answers.at[slot, g],
            dst_ref=returned.at[server, g],
            send_sem=back_send.at[slot, g],
            recv_sem=back_recv.at[server, g],
            device_id={"srv": slot},
            device_id_type=MESH,
        )

    half = block_rows // 2

    def kv_copy(source, target, slot, hop, chunk, sent):
        low = hop * block_rows + chunk % 2 * half
        return pltpu.make_async_remote_copy(
            src_ref=source[chunk // 2].at[pl.ds(slot * block_rows + chunk % 2 * half, half)],
            dst_ref=(keys, values)[chunk // 2].at[pl.ds(low, half)],
            send_sem=sent.at[chunk],
            recv_sem=kv_recv.at[hop - 1, chunk],
            device_id={"blk": target},
            device_id_type=MESH,
        )

    own = (key_rows.at[0], value_rows.at[0])
    held = (keys, values)
    is_odd = lax.rem(blk, 2) == 1
    has_two = blk >= 2
    by_relay = is_odd & (blk + 2 < blocks)
    to_one = (blk + 1 < blocks) & jnp.logical_not(by_relay)

    def own_one(chunk):
        return kv_copy(own, blk + 1, 0, 1, chunk, own_send.at[0])

    def own_two(chunk):
        return kv_copy(own, blk + 2, 0, 2, chunk, own_send.at[1])

    def relay_back(chunk):
        return kv_copy(held, blk - 1, 2, 1, chunk, relay_send.at[0])

    def relay_on(chunk):
        return kv_copy(held, blk + 1, 2, 3, chunk, relay_send.at[1])

    def arrived(hop, chunk):
        return kv_copy(held, blk, 0, hop, chunk, own_send.at[0])

    def pass_on(chunk):
        @pl.when(has_two)
        def _():
            arrived(2, chunk).wait_recv()

        @pl.when(has_two & (blk + 1 < blocks))
        def _():
            relay_on(chunk).start()

        @pl.when(has_two & is_odd)
        def _():
            relay_back(chunk).start()

    def send_queries(step):
        peer = lax.rem(me + 1 + step, servers)
        query_copy(peer, me).start()
        place_copy(peer, me).start()

    each(servers - 1, send_queries)
    for chunk in range(CHUNKS):

        @pl.when(blk + 2 < blocks)
        def _():
            own_two(chunk).start()

        @pl.when(to_one)
        def _():
            own_one(chunk).start()

    query_in[me] = query_out[me]
    place_in[me] = place_out[me]
    load_keys.wait()

    def score(slot, hop):
        for g in range(KVH):
            block = keys[pl.ds(hop * block_rows, block_rows), g * HD : (g + 1) * HD]
            scores[slot, g, :, hop * block_rows : (hop + 1) * block_rows] = lax.dot_general(
                query_in[slot, g],
                block,
                (((1,), (1,)), ((), ())),
                preferred_element_type=jnp.float32,
            )

    score(me, 0)
    pass_on(0)
    pass_on(1)

    def first_scores(step):
        peer = lax.rem(me + 1 + step, servers)
        query_copy(peer, peer).wait_recv()
        place_copy(peer, peer).wait_recv()
        score(peer, 0)

    each(servers - 1, first_scores)
    each(servers, lambda slot: score(slot, 2))
    for chunk in range(CHUNKS // 2, CHUNKS):
        pass_on(chunk)
    for hop in (1, 3):

        @pl.when(blk >= hop)
        def _():
            for chunk in range(CHUNKS // 2):
                arrived(hop, chunk).wait_recv()

        each(servers, lambda slot: score(slot, hop))
    load_values.wait()
    for hop in (1, 3):

        @pl.when(blk >= hop)
        def _():
            for chunk in range(CHUNKS // 2, CHUNKS):
                arrived(hop, chunk).wait_recv()

    ends = []
    running = jnp.int32(0)
    for doc in range(docs):
        running = running + lengths[0, doc]
        ends.append(running)
    lane = lax.broadcasted_iota(jnp.int32, (slot_rows, LANES), 1)

    def attend(slot, g):
        place = place_in[slot]
        first = jnp.zeros_like(place)
        for end in ends:
            first = jnp.where(end <= place, end, first)
        pieces = []
        highest = None
        for hop in range(BACK + 1):
            for part in range(block_rows // LANES):
                low = hop * block_rows + part * LANES
                at = (blk - hop) * block_rows + part * LANES + lane
                allowed = (at <= place) & (at >= first)
                piece = scores[slot, g, :, low : low + LANES] * scaling
                piece = piece.reshape(groups, slot_rows, LANES)
                piece = jnp.where(allowed[None], piece, -1e30)
                pieces.append(piece)
                highest = piece if highest is None else jnp.maximum(highest, piece)
        highest = jnp.max(highest, axis=2, keepdims=True)
        weights = [jnp.exp(piece - highest) for piece in pieces]
        total = weights[0]
        for weight in weights[1:]:
            total = total + weight
        total = jnp.sum(total, axis=2, keepdims=True)
        joined = jnp.concatenate(
            [w.reshape(head_rows, LANES).astype(jnp.bfloat16) for w in weights], axis=1
        )
        weighted = jnp.dot(
            joined, values[:, g * HD : (g + 1) * HD], preferred_element_type=jnp.float32
        )
        return (weighted / total.reshape(head_rows, 1)).astype(jnp.bfloat16)

    def serve(step):
        peer = lax.rem(me + 1 + step, servers)
        for g in range(KVH):
            answers[peer, g] = attend(peer, g)
            back_copy(peer, g, me).start()

    each(servers - 1, serve)
    for g in range(KVH):
        returned[me, g] = attend(me, g)

    def collect(step):
        peer = lax.rem(me + 1 + step, servers)
        for g in range(KVH):
            back_copy(peer, g, peer).wait_recv()

    each(servers - 1, collect)

    out_row = lax.broadcasted_iota(jnp.int32, (tasks * R, servers * slot_rows), 0)
    from_row = lax.broadcasted_iota(jnp.int32, (tasks * R, servers * slot_rows), 1)
    row_target = jnp.full((tasks * R, servers * slot_rows), -1, jnp.int32)
    for task in range(tasks):
        row_target = jnp.where(out_row // R == task, destination[0, 0, task], row_target)
    within = from_row % slot_rows
    taken = (
        (row_target == from_row // slot_rows)
        & (within // R == out_row // (per_round * R))
        & (within % R == out_row % R)
    )
    taken = jnp.where(taken, 1.0, 0.0).astype(jnp.bfloat16)
    for g in range(KVH):
        got = [returned[slot, g].astype(jnp.float32) for slot in range(servers)]
        wide = []
        for h in range(groups):
            stacked = [piece[h * slot_rows : (h + 1) * slot_rows] for piece in got]
            wide.append(jnp.concatenate(stacked, axis=0).astype(jnp.bfloat16))
        wide = jnp.concatenate(wide, axis=1)
        out[0, 0, :, g * groups * HD : (g + 1) * groups * HD] = jnp.dot(
            taken, wide, preferred_element_type=jnp.float32
        ).astype(jnp.bfloat16)

    def finish(step):
        peer = lax.rem(me + 1 + step, servers)
        query_copy(peer, me).wait_send()
        place_copy(peer, me).wait_send()
        for g in range(KVH):
            back_copy(peer, g, me).wait_send()

    each(servers - 1, finish)
    for chunk in range(CHUNKS):

        @pl.when(blk + 2 < blocks)
        def _():
            own_two(chunk).wait_send()

        @pl.when(to_one)
        def _():
            own_one(chunk).wait_send()

        @pl.when(has_two & (blk + 1 < blocks))
        def _():
            relay_on(chunk).wait_send()

        @pl.when(has_two & is_odd)
        def _():
            relay_back(chunk).wait_send()


def solution(mesh):
    servers = mesh.shape["srv"]
    blocks = mesh.shape["blk"]
    placed = (
        P("srv", "blk", "rep", None),
        P("srv", "blk", "rep"),
        P("srv", "blk", "rep"),
        P("srv", "blk", "rep"),
        P("srv", "blk", "rep"),
        P("srv", "rep"),
    )

    def on_device(queries, destination, offsets, key_rows, value_rows, lengths):
        block_rows, kv_width = key_rows.shape[1:]
        slot_rows = ROUNDS * R
        packed = (servers, KVH, QH // KVH * slot_rows, HD)
        window = (BACK + 1) * block_rows
        smem = pl.BlockSpec(memory_space=pltpu.SMEM)
        anywhere = pl.BlockSpec(memory_space=pl.ANY)
        dma = pltpu.SemaphoreType.DMA

        def body(*refs):
            kernel(servers, blocks, *refs)

        return pl.pallas_call(
            body,
            name="routed_attention",
            out_shape=pltpu.VMEM(queries.shape, queries.dtype),
            in_specs=[smem] * 3 + [anywhere] * 3,
            out_specs=pl.BlockSpec(memory_space=pltpu.VMEM),
            scratch_shapes=[
                pltpu.VMEM(queries.shape[2:], jnp.bfloat16),
                pltpu.VMEM((window, kv_width), jnp.bfloat16),
                pltpu.VMEM((window, kv_width), jnp.bfloat16),
                pltpu.VMEM(packed, jnp.bfloat16),
                pltpu.VMEM(packed, jnp.bfloat16),
                pltpu.VMEM((servers, slot_rows, LANES), jnp.int32),
                pltpu.VMEM((servers, slot_rows, LANES), jnp.int32),
                pltpu.VMEM(packed[:3] + (window,), jnp.float32),
                pltpu.VMEM(packed, jnp.bfloat16),
                pltpu.VMEM(packed, jnp.bfloat16),
                dma((3,)),
                dma((2, CHUNKS)),
                dma((2, CHUNKS)),
                dma((BACK, CHUNKS)),
                dma((servers,)),
                dma((servers,)),
                dma((servers,)),
                dma((servers,)),
                dma((servers, KVH)),
                dma((servers, KVH)),
            ],
            compiler_params=pltpu.CompilerParams(collective_id=0, has_side_effects=True),
        )(destination, offsets, lengths, queries, key_rows, value_rows)

    return jax.shard_map(
        on_device,
        mesh=mesh,
        in_specs=placed,
        out_specs=P("srv", "blk", "rep", None),
        check_vma=False,
    )
```

```python
import math

import jax
import jax.numpy as jnp
from jax import lax
from jax.experimental import pallas as pl
from jax.experimental.pallas import tpu as pltpu
from jax.sharding import PartitionSpec as P

QH = 32
KVH = 2
HD = 128
R = 4
ROUNDS = 2
BACK = 3
CHUNKS = 4
LANES = 128
MESH = pl.DeviceIdType.MESH


def each(count, body):
    if count <= 2:
        for index in range(count):
            body(index)
    else:
        lax.fori_loop(0, count, lambda index, carry: (body(index), carry)[1], 0)


def kernel(
    servers,
    blocks,
    destination,
    offsets,
    lengths,
    queries,
    key_rows,
    value_rows,
    out,
    own_queries,
    keys,
    values,
    query_out,
    query_in,
    place_out,
    place_in,
    scores,
    weights,
    totals,
    answers,
    returned,
    load_sem,
    own_send,
    relay_send,
    kv_recv,
    query_send,
    query_recv,
    place_send,
    place_recv,
    back_send,
    back_recv,
):
    me = lax.axis_index("srv")
    blk = lax.axis_index("blk")
    block_rows = key_rows.shape[1]
    tasks = destination.shape[2]
    per_round = tasks // ROUNDS
    groups = QH // KVH
    slot_rows = ROUNDS * R
    head_rows = groups * slot_rows
    scaling = 1.0 / math.sqrt(HD)
    docs = lengths.shape[1]

    load_queries = pltpu.make_async_copy(queries.at[0, 0], own_queries, load_sem.at[0])
    load_keys = pltpu.make_async_copy(
        key_rows.at[0], keys.at[pl.ds(0, block_rows)], load_sem.at[1]
    )
    load_values = pltpu.make_async_copy(
        value_rows.at[0], values.at[pl.ds(0, block_rows)], load_sem.at[2]
    )
    load_queries.start()
    load_keys.start()
    load_values.start()

    barrier = pltpu.get_barrier_semaphore()
    for hop in range(1, BACK):

        @pl.when(blk + hop < blocks)
        def _():
            pl.semaphore_signal(
                barrier, inc=1, device_id={"blk": blk + hop}, device_id_type=MESH
            )

        @pl.when(blk >= hop)
        def _():
            pl.semaphore_signal(
                barrier, inc=1, device_id={"blk": blk - hop}, device_id_type=MESH
            )

    def greet(step):
        peer = lax.rem(me + 1 + step, servers)
        pl.semaphore_signal(barrier, inc=1, device_id={"srv": peer}, device_id_type=MESH)

    each(servers - 1, greet)

    for hop in range(1, BACK + 1):

        @pl.when(blk < hop)
        def _():
            empty = jnp.zeros((block_rows, keys.shape[1]), keys.dtype)
            keys[pl.ds(hop * block_rows, block_rows), :] = empty
            values[pl.ds(hop * block_rows, block_rows), :] = empty

    load_queries.wait()
    all_rows = own_queries[...]
    row = lax.broadcasted_iota(jnp.int32, (slot_rows, tasks * R), 0)
    column = lax.broadcasted_iota(jnp.int32, (slot_rows, tasks * R), 1)
    column_target = jnp.full((slot_rows, tasks * R), -1, jnp.int32)
    for task in range(tasks):
        column_target = jnp.where(
            column // R == task, destination[0, 0, task], column_target
        )
    same_place = (row // R == column // (per_round * R)) & (row % R == column % R)
    place_row = lax.broadcasted_iota(jnp.int32, (slot_rows, LANES), 0)

    def pack(slot):
        chosen = jnp.where(same_place & (column_target == slot), 1.0, 0.0).astype(jnp.bfloat16)
        routed = jnp.dot(chosen, all_rows, preferred_element_type=jnp.float32)
        for g in range(KVH):
            parts = [
                routed[:, (g * groups + h) * HD : (g * groups + h + 1) * HD]
                for h in range(groups)
            ]
            query_out[slot, g] = jnp.concatenate(parts, axis=0).astype(jnp.bfloat16)
        start = jnp.zeros((slot_rows, LANES), jnp.int32)
        for turn in range(ROUNDS):
            offset = jnp.int32(0)
            for t in range(per_round):
                task = turn * per_round + t
                offset = jnp.where(
                    destination[0, 0, task] == slot, offsets[0, 0, task], offset
                )
            start = jnp.where(place_row // R == turn, offset, start)
        place_out[slot] = start + place_row % R + blk * block_rows

    each(servers, pack)

    neighbours = (
        jnp.minimum(blk, BACK - 1)
        + jnp.minimum(blocks - 1 - blk, BACK - 1)
        + (servers - 1)
    )
    pl.semaphore_wait(barrier, neighbours)

    def query_copy(slot, source):
        return pltpu.make_async_remote_copy(
            src_ref=query_out.at[slot],
            dst_ref=query_in.at[source],
            send_sem=query_send.at[slot],
            recv_sem=query_recv.at[source],
            device_id={"srv": slot},
            device_id_type=MESH,
        )

    def place_copy(slot, source):
        return pltpu.make_async_remote_copy(
            src_ref=place_out.at[slot],
            dst_ref=place_in.at[source],
            send_sem=place_send.at[slot],
            recv_sem=place_recv.at[source],
            device_id={"srv": slot},
            device_id_type=MESH,
        )

    def back_copy(slot, g, server):
        return pltpu.make_async_remote_copy(
            src_ref=answers.at[slot, g],
            dst_ref=returned.at[server, g],
            send_sem=back_send.at[slot, g],
            recv_sem=back_recv.at[server, g],
            device_id={"srv": slot},
            device_id_type=MESH,
        )

    pieces = CHUNKS // 2
    part_rows = block_rows // pieces

    def kv_copy(source, target, slot, hop, chunk, sent):
        part = chunk % pieces * part_rows
        low = hop * block_rows + part
        return pltpu.make_async_remote_copy(
            src_ref=source[chunk // pieces].at[pl.ds(slot * block_rows + part, part_rows)],
            dst_ref=(keys, values)[chunk // pieces].at[pl.ds(low, part_rows)],
            send_sem=sent.at[chunk],
            recv_sem=kv_recv.at[hop - 1, chunk],
            device_id={"blk": target},
            device_id_type=MESH,
        )

    own = (key_rows.at[0], value_rows.at[0])
    held = (keys, values)
    is_odd = lax.rem(blk, 2) == 1
    relays = (blk >= 2) & jnp.logical_not(is_odd)
    has_one = blk + 1 < blocks
    has_next = blk + 2 < blocks

    def own_one(chunk):
        return kv_copy(own, blk + 1, 0, 1, chunk, own_send.at[0])

    def own_two(chunk):
        return kv_copy(own, blk + 2, 0, 2, chunk, own_send.at[1])

    def relay_on(chunk):
        return kv_copy(held, blk + 1, 2, 3, chunk, relay_send.at[0])

    def arrived(hop, chunk):
        return kv_copy(held, blk, 0, hop, chunk, own_send.at[0])

    def relay_two(chunk):
        return kv_copy(held, blk + 2, 1, 3, chunk, relay_send.at[1])

    def await_all(hop, chunks):
        for chunk in chunks:
            arrived(hop, chunk).wait_recv()

    def take_two(chunk):
        arrived(2, chunk).wait_recv()

        @pl.when(has_one)
        def _():
            relay_on(chunk).start()

    def take_one(chunk):
        arrived(1, chunk).wait_recv()

        @pl.when(has_next)
        def _():
            relay_two(chunk).start()

    def send_queries(step):
        peer = lax.rem(me + 1 + step, servers)
        query_copy(peer, me).start()
        place_copy(peer, me).start()

    each(servers - 1, send_queries)
    @pl.when(has_one)
    def _():
        for chunk in range(CHUNKS):
            own_one(chunk).start()

    @pl.when(has_next)
    def _():
        for chunk in range(CHUNKS):
            own_two(chunk).start()

    query_in[me] = query_out[me]
    place_in[me] = place_out[me]
    load_keys.wait()

    def score(slot, hop):
        for g in range(KVH):
            block = keys[pl.ds(hop * block_rows, block_rows), g * HD : (g + 1) * HD]
            scores[slot, g, :, hop * block_rows : (hop + 1) * block_rows] = lax.dot_general(
                query_in[slot, g],
                block,
                (((1,), (1,)), ((), ())),
                preferred_element_type=jnp.float32,
            )

    score(me, 0)
    @pl.when(relays)
    def _():
        take_two(0)
        for chunk in range(CHUNKS):
            if chunk + 1 < CHUNKS:
                take_two(chunk + 1)
            take_one(chunk)

    def first_scores(step):
        peer = lax.rem(me + 1 + step, servers)
        query_copy(peer, peer).wait_recv()
        place_copy(peer, peer).wait_recv()
        score(peer, 0)

    each(servers - 1, first_scores)
    first_half, second_half = range(pieces), range(pieces, CHUNKS)

    @pl.when(is_odd)
    def _():
        await_all(1, first_half)

    each(servers, lambda slot: score(slot, 1))

    @pl.when(is_odd & (blk >= 2))
    def _():
        await_all(2, first_half)

    each(servers, lambda slot: score(slot, 2))

    @pl.when(blk >= 3)
    def _():
        await_all(3, first_half)

    each(servers, lambda slot: score(slot, 3))

    ends = []
    running = jnp.int32(0)
    for doc in range(docs):
        running = running + lengths[0, doc]
        ends.append(running)
    lane = lax.broadcasted_iota(jnp.int32, (slot_rows, LANES), 1)

    def weigh(slot):
        place = place_in[slot]
        first = jnp.zeros_like(place)
        for end in ends:
            first = jnp.where(end <= place, end, first)
        for g in range(KVH):
            logits = []
            highest = None
            for low in range(0, (BACK + 1) * block_rows, LANES):
                hop = low // block_rows
                at = (blk - hop) * block_rows + low % block_rows + lane
                allowed = (at <= place) & (at >= first)
                piece = scores[slot, g, :, low : low + LANES] * scaling
                piece = piece.reshape(groups, slot_rows, LANES)
                piece = jnp.where(allowed[None], piece, -1e30)
                logits.append(piece)
                highest = piece if highest is None else jnp.maximum(highest, piece)
            highest = jnp.max(highest, axis=2, keepdims=True)
            total = None
            for index, piece in enumerate(logits):
                weight = jnp.exp(piece - highest)
                total = weight if total is None else total + weight
                weights[slot, g, :, index * LANES : (index + 1) * LANES] = weight.reshape(
                    head_rows, LANES
                ).astype(jnp.bfloat16)
            total = jnp.sum(total, axis=2, keepdims=True).reshape(head_rows, 1)
            totals[slot, g] = jnp.broadcast_to(total, (head_rows, HD))

    def attend(slot, g):
        weighted = jnp.dot(
            weights[slot, g],
            values[:, g * HD : (g + 1) * HD],
            preferred_element_type=jnp.float32,
        )
        return (weighted / totals[slot, g]).astype(jnp.bfloat16)

    each(servers, weigh)
    load_values.wait()

    @pl.when(is_odd)
    def _():
        await_all(1, second_half)

    @pl.when(is_odd & (blk >= 2))
    def _():
        await_all(2, second_half)

    @pl.when(blk >= 3)
    def _():
        await_all(3, second_half)

    def serve(step):
        peer = lax.rem(me + 1 + step, servers)
        for g in range(KVH):
            answers[peer, g] = attend(peer, g)
            back_copy(peer, g, me).start()

    each(servers - 1, serve)
    for g in range(KVH):
        returned[me, g] = attend(me, g)

    def collect(step):
        peer = lax.rem(me + 1 + step, servers)
        for g in range(KVH):
            back_copy(peer, g, peer).wait_recv()

    each(servers - 1, collect)

    out_row = lax.broadcasted_iota(jnp.int32, (tasks * R, servers * slot_rows), 0)
    from_row = lax.broadcasted_iota(jnp.int32, (tasks * R, servers * slot_rows), 1)
    row_target = jnp.full((tasks * R, servers * slot_rows), -1, jnp.int32)
    for task in range(tasks):
        row_target = jnp.where(out_row // R == task, destination[0, 0, task], row_target)
    within = from_row % slot_rows
    taken = (
        (row_target == from_row // slot_rows)
        & (within // R == out_row // (per_round * R))
        & (within % R == out_row % R)
    )
    taken = jnp.where(taken, 1.0, 0.0).astype(jnp.bfloat16)
    for g in range(KVH):
        got = [returned[slot, g].astype(jnp.float32) for slot in range(servers)]
        wide = []
        for h in range(groups):
            stacked = [piece[h * slot_rows : (h + 1) * slot_rows] for piece in got]
            wide.append(jnp.concatenate(stacked, axis=0).astype(jnp.bfloat16))
        wide = jnp.concatenate(wide, axis=1)
        out[0, 0, :, g * groups * HD : (g + 1) * groups * HD] = jnp.dot(
            taken, wide, preferred_element_type=jnp.float32
        ).astype(jnp.bfloat16)

    def finish(step):
        peer = lax.rem(me + 1 + step, servers)
        query_copy(peer, me).wait_send()
        place_copy(peer, me).wait_send()
        for g in range(KVH):
            back_copy(peer, g, me).wait_send()

    each(servers - 1, finish)
    @pl.when(has_one)
    def _():
        for chunk in range(CHUNKS):
            own_one(chunk).wait_send()

    @pl.when(has_next)
    def _():
        for chunk in range(CHUNKS):
            own_two(chunk).wait_send()

    @pl.when(relays & has_one)
    def _():
        for chunk in range(CHUNKS):
            relay_on(chunk).wait_send()

    @pl.when(relays & has_next)
    def _():
        for chunk in range(CHUNKS):
            relay_two(chunk).wait_send()


def solution(mesh):
    servers = mesh.shape["srv"]
    blocks = mesh.shape["blk"]
    placed = (
        P("srv", "blk", "rep", None),
        P("srv", "blk", "rep"),
        P("srv", "blk", "rep"),
        P("srv", "blk", "rep"),
        P("srv", "blk", "rep"),
        P("srv", "rep"),
    )

    def on_device(queries, destination, offsets, key_rows, value_rows, lengths):
        block_rows, kv_width = key_rows.shape[1:]
        slot_rows = ROUNDS * R
        packed = (servers, KVH, QH // KVH * slot_rows, HD)
        window = (BACK + 1) * block_rows
        smem = pl.BlockSpec(memory_space=pltpu.SMEM)
        anywhere = pl.BlockSpec(memory_space=pl.ANY)
        dma = pltpu.SemaphoreType.DMA

        def body(*refs):
            kernel(servers, blocks, *refs)

        return pl.pallas_call(
            body,
            name="routed_attention",
            out_shape=pltpu.VMEM(queries.shape, queries.dtype),
            in_specs=[smem] * 3 + [anywhere] * 3,
            out_specs=pl.BlockSpec(memory_space=pltpu.VMEM),
            scratch_shapes=[
                pltpu.VMEM(queries.shape[2:], jnp.bfloat16),
                pltpu.VMEM((window, kv_width), jnp.bfloat16),
                pltpu.VMEM((window, kv_width), jnp.bfloat16),
                pltpu.VMEM(packed, jnp.bfloat16),
                pltpu.VMEM(packed, jnp.bfloat16),
                pltpu.VMEM((servers, slot_rows, LANES), jnp.int32),
                pltpu.VMEM((servers, slot_rows, LANES), jnp.int32),
                pltpu.VMEM(packed[:3] + (window,), jnp.float32),
                pltpu.VMEM(packed[:3] + (window,), jnp.bfloat16),
                pltpu.VMEM(packed, jnp.float32),
                pltpu.VMEM(packed, jnp.bfloat16),
                pltpu.VMEM(packed, jnp.bfloat16),
                dma((3,)),
                dma((2, CHUNKS)),
                dma((2, CHUNKS)),
                dma((BACK, CHUNKS)),
                dma((servers,)),
                dma((servers,)),
                dma((servers,)),
                dma((servers,)),
                dma((servers, KVH)),
                dma((servers, KVH)),
            ],
            compiler_params=pltpu.CompilerParams(collective_id=0, has_side_effects=True),
        )(destination, offsets, lengths, queries, key_rows, value_rows)

    return jax.shard_map(
        on_device,
        mesh=mesh,
        in_specs=placed,
        out_specs=P("srv", "blk", "rep", None),
        check_vma=False,
    )
```

```python
import math

import jax
import jax.numpy as jnp
from jax import lax
from jax.experimental import pallas as pl
from jax.experimental.pallas import tpu as pltpu
from jax.sharding import PartitionSpec as P

QH = 32
KVH = 2
HD = 128
R = 4
ROUNDS = 2
BACK = 3
CHUNKS = 4
LANES = 128
MESH = pl.DeviceIdType.MESH


def each(count, body):
    if count <= 2:
        for index in range(count):
            body(index)
    else:
        lax.fori_loop(0, count, lambda index, carry: (body(index), carry)[1], 0)


def kernel(
    servers,
    blocks,
    destination,
    offsets,
    lengths,
    queries,
    key_rows,
    value_rows,
    out,
    own_queries,
    keys,
    values,
    query_out,
    query_in,
    place_out,
    place_in,
    scores,
    weights,
    totals,
    gathered,
    answers,
    returned,
    load_sem,
    own_send,
    relay_send,
    kv_recv,
    query_send,
    query_recv,
    place_send,
    place_recv,
    back_send,
    back_recv,
):
    me = lax.axis_index("srv")
    blk = lax.axis_index("blk")
    block_rows = key_rows.shape[1]
    tasks = destination.shape[2]
    per_round = tasks // ROUNDS
    groups = QH // KVH
    slot_rows = ROUNDS * R
    head_rows = groups * slot_rows
    scaling = 1.0 / math.sqrt(HD)
    docs = lengths.shape[1]

    load_queries = pltpu.make_async_copy(queries.at[0, 0], own_queries, load_sem.at[0])
    load_keys = pltpu.make_async_copy(
        key_rows.at[0], keys.at[pl.ds(0, block_rows)], load_sem.at[1]
    )
    load_values = pltpu.make_async_copy(
        value_rows.at[0], values.at[pl.ds(0, block_rows)], load_sem.at[2]
    )
    load_queries.start()
    load_keys.start()
    load_values.start()

    barrier = pltpu.get_barrier_semaphore()
    for hop in range(1, BACK):

        @pl.when(blk + hop < blocks)
        def _():
            pl.semaphore_signal(
                barrier, inc=1, device_id={"blk": blk + hop}, device_id_type=MESH
            )

        @pl.when(blk >= hop)
        def _():
            pl.semaphore_signal(
                barrier, inc=1, device_id={"blk": blk - hop}, device_id_type=MESH
            )

    def greet(step):
        peer = lax.rem(me + 1 + step, servers)
        pl.semaphore_signal(barrier, inc=1, device_id={"srv": peer}, device_id_type=MESH)

    each(servers - 1, greet)

    for hop in range(1, BACK + 1):

        @pl.when(blk < hop)
        def _():
            empty = jnp.zeros((block_rows, keys.shape[1]), keys.dtype)
            keys[pl.ds(hop * block_rows, block_rows), :] = empty
            values[pl.ds(hop * block_rows, block_rows), :] = empty

    load_queries.wait()
    all_rows = own_queries[...]
    row = lax.broadcasted_iota(jnp.int32, (slot_rows, tasks * R), 0)
    column = lax.broadcasted_iota(jnp.int32, (slot_rows, tasks * R), 1)
    column_target = jnp.full((slot_rows, tasks * R), -1, jnp.int32)
    for task in range(tasks):
        column_target = jnp.where(
            column // R == task, destination[0, 0, task], column_target
        )
    same_place = (row // R == column // (per_round * R)) & (row % R == column % R)
    place_row = lax.broadcasted_iota(jnp.int32, (slot_rows, LANES), 0)

    def pack(slot):
        chosen = jnp.where(same_place & (column_target == slot), 1.0, 0.0).astype(jnp.bfloat16)
        routed = jnp.dot(chosen, all_rows, preferred_element_type=jnp.float32)
        for g in range(KVH):
            parts = [
                routed[:, (g * groups + h) * HD : (g * groups + h + 1) * HD]
                for h in range(groups)
            ]
            query_out[slot, g] = jnp.concatenate(parts, axis=0).astype(jnp.bfloat16)
        start = jnp.zeros((slot_rows, LANES), jnp.int32)
        for turn in range(ROUNDS):
            offset = jnp.int32(0)
            for t in range(per_round):
                task = turn * per_round + t
                offset = jnp.where(
                    destination[0, 0, task] == slot, offsets[0, 0, task], offset
                )
            start = jnp.where(place_row // R == turn, offset, start)
        place_out[slot] = start + place_row % R + blk * block_rows

    each(servers, pack)

    neighbours = (
        jnp.minimum(blk, BACK - 1)
        + jnp.minimum(blocks - 1 - blk, BACK - 1)
        + (servers - 1)
    )
    pl.semaphore_wait(barrier, neighbours)

    def query_copy(slot, source):
        return pltpu.make_async_remote_copy(
            src_ref=query_out.at[slot],
            dst_ref=query_in.at[source],
            send_sem=query_send.at[slot],
            recv_sem=query_recv.at[source],
            device_id={"srv": slot},
            device_id_type=MESH,
        )

    def place_copy(slot, source):
        return pltpu.make_async_remote_copy(
            src_ref=place_out.at[slot],
            dst_ref=place_in.at[source],
            send_sem=place_send.at[slot],
            recv_sem=place_recv.at[source],
            device_id={"srv": slot},
            device_id_type=MESH,
        )

    def back_copy(slot, g, server):
        return pltpu.make_async_remote_copy(
            src_ref=answers.at[slot, g],
            dst_ref=returned.at[server, g],
            send_sem=back_send.at[slot, g],
            recv_sem=back_recv.at[server, g],
            device_id={"srv": slot},
            device_id_type=MESH,
        )

    pieces = CHUNKS // 2
    part_rows = block_rows // pieces

    def kv_copy(source, target, slot, hop, chunk, sent):
        part = chunk % pieces * part_rows
        low = hop * block_rows + part
        return pltpu.make_async_remote_copy(
            src_ref=source[chunk // pieces].at[pl.ds(slot * block_rows + part, part_rows)],
            dst_ref=(keys, values)[chunk // pieces].at[pl.ds(low, part_rows)],
            send_sem=sent.at[chunk],
            recv_sem=kv_recv.at[hop - 1, chunk],
            device_id={"blk": target},
            device_id_type=MESH,
        )

    own = (key_rows.at[0], value_rows.at[0])
    held = (keys, values)
    is_odd = lax.rem(blk, 2) == 1
    relays = (blk >= 2) & jnp.logical_not(is_odd)
    late = is_odd & (lax.axis_index("rep") == 1)
    has_one = blk + 1 < blocks
    has_next = blk + 2 < blocks

    def own_one(chunk):
        return kv_copy(own, blk + 1, 0, 1, chunk, own_send.at[0])

    def own_two(chunk):
        return kv_copy(own, blk + 2, 0, 2, chunk, own_send.at[1])

    def relay_on(chunk):
        return kv_copy(held, blk + 1, 2, 3, chunk, relay_send.at[0])

    def arrived(hop, chunk):
        return kv_copy(held, blk, 0, hop, chunk, own_send.at[0])

    def relay_two(chunk):
        return kv_copy(held, blk + 2, 1, 3, chunk, relay_send.at[1])

    def await_all(hop, chunks):
        for chunk in chunks:
            arrived(hop, chunk).wait_recv()

    def take_two(chunk):
        arrived(2, chunk).wait_recv()

        @pl.when(has_one)
        def _():
            relay_on(chunk).start()

    def take_one(chunk):
        arrived(1, chunk).wait_recv()

        @pl.when(has_next)
        def _():
            relay_two(chunk).start()

    def send_queries(step):
        peer = lax.rem(me + 1 + step, servers)
        query_copy(peer, me).start()
        place_copy(peer, me).start()

    each(servers - 1, send_queries)
    @pl.when(has_one)
    def _():
        for chunk in range(CHUNKS):
            own_one(chunk).start()

    @pl.when(has_next & jnp.logical_not(late))
    def _():
        for chunk in range(CHUNKS):
            own_two(chunk).start()

    query_in[me] = query_out[me]
    place_in[me] = place_out[me]
    load_keys.wait()

    def score(slot, hop):
        for g in range(KVH):
            block = keys[pl.ds(hop * block_rows, block_rows), g * HD : (g + 1) * HD]
            scores[slot, g, :, hop * block_rows : (hop + 1) * block_rows] = lax.dot_general(
                query_in[slot, g],
                block,
                (((1,), (1,)), ((), ())),
                preferred_element_type=jnp.float32,
            )

    score(me, 0)
    first_half, second_half = range(pieces), range(pieces, CHUNKS)

    @pl.when(is_odd)
    def _():
        await_all(1, first_half)

    @pl.when(late)
    def _():
        await_all(1, second_half)

    @pl.when(has_next & late)
    def _():
        for chunk in range(CHUNKS):
            own_two(chunk).start()

    @pl.when(relays)
    def _():
        take_two(0)
        for chunk in range(CHUNKS):
            if chunk + 1 < CHUNKS:
                take_two(chunk + 1)
            take_one(chunk)

    def first_scores(step):
        peer = lax.rem(me + 1 + step, servers)
        query_copy(peer, peer).wait_recv()
        place_copy(peer, peer).wait_recv()
        score(peer, 0)

    each(servers - 1, first_scores)
    each(servers, lambda slot: score(slot, 1))

    @pl.when(is_odd & (blk >= 2))
    def _():
        await_all(2, first_half)

    each(servers, lambda slot: score(slot, 2))

    @pl.when(blk >= 3)
    def _():
        await_all(3, first_half)

    each(servers, lambda slot: score(slot, 3))

    ends = []
    running = jnp.int32(0)
    for doc in range(docs):
        running = running + lengths[0, doc]
        ends.append(running)
    lane = lax.broadcasted_iota(jnp.int32, (slot_rows, LANES), 1)

    def weigh(slot):
        place = place_in[slot]
        first = jnp.zeros_like(place)
        for end in ends:
            first = jnp.where(end <= place, end, first)
        for g in range(KVH):
            logits = []
            highest = None
            for low in range(0, (BACK + 1) * block_rows, LANES):
                hop = low // block_rows
                at = (blk - hop) * block_rows + low % block_rows + lane
                allowed = (at <= place) & (at >= first)
                piece = scores[slot, g, :, low : low + LANES] * scaling
                piece = piece.reshape(groups, slot_rows, LANES)
                piece = jnp.where(allowed[None], piece, -1e30)
                logits.append(piece)
                highest = piece if highest is None else jnp.maximum(highest, piece)
            highest = jnp.max(highest, axis=2, keepdims=True)
            total = None
            for index, piece in enumerate(logits):
                weight = jnp.exp(piece - highest)
                total = weight if total is None else total + weight
                weights[slot, g, :, index * LANES : (index + 1) * LANES] = weight.reshape(
                    head_rows, LANES
                ).astype(jnp.bfloat16)
            total = jnp.sum(total, axis=2, keepdims=True).reshape(head_rows, 1)
            totals[slot, g] = jnp.broadcast_to(total, (head_rows, HD))

    def attend(slot, g):
        weighted = jnp.dot(
            weights[slot, g],
            values[:, g * HD : (g + 1) * HD],
            preferred_element_type=jnp.float32,
        )
        return (weighted / totals[slot, g]).astype(jnp.bfloat16)

    each(servers, weigh)
    load_values.wait()

    @pl.when(is_odd & jnp.logical_not(late))
    def _():
        await_all(1, second_half)

    @pl.when(is_odd & (blk >= 2))
    def _():
        await_all(2, second_half)

    @pl.when(blk >= 3)
    def _():
        await_all(3, second_half)

    def serve(step):
        peer = lax.rem(me + 1 + step, servers)
        for g in range(KVH):
            answers[peer, g] = attend(peer, g)
            back_copy(peer, g, me).start()

    each(servers - 1, serve)
    for g in range(KVH):
        returned[me, g] = attend(me, g)

    out_row = lax.broadcasted_iota(jnp.int32, (tasks * R, slot_rows), 0)
    from_row = lax.broadcasted_iota(jnp.int32, (tasks * R, slot_rows), 1)
    row_target = jnp.full((tasks * R, slot_rows), -1, jnp.int32)
    for task in range(tasks):
        row_target = jnp.where(out_row // R == task, destination[0, 0, task], row_target)
    aligned = (from_row // R == out_row // (per_round * R)) & (from_row % R == out_row % R)

    def unpack(slot, g):
        taken = jnp.where(aligned & (row_target == slot), 1.0, 0.0).astype(jnp.bfloat16)
        got = returned[slot, g].astype(jnp.float32)
        wide = [got[h * slot_rows : (h + 1) * slot_rows] for h in range(groups)]
        wide = jnp.concatenate(wide, axis=1).astype(jnp.bfloat16)
        return jnp.dot(taken, wide, preferred_element_type=jnp.float32)

    for g in range(KVH):
        gathered[g] = unpack(me, g)

    def collect(step):
        peer = lax.rem(me + 1 + step, servers)
        for g in range(KVH):
            back_copy(peer, g, peer).wait_recv()
            gathered[g] += unpack(peer, g)

    each(servers - 1, collect)
    for g in range(KVH):
        out[0, 0, :, g * groups * HD : (g + 1) * groups * HD] = gathered[g].astype(jnp.bfloat16)

    def finish(step):
        peer = lax.rem(me + 1 + step, servers)
        query_copy(peer, me).wait_send()
        place_copy(peer, me).wait_send()
        for g in range(KVH):
            back_copy(peer, g, me).wait_send()

    each(servers - 1, finish)
    @pl.when(has_one)
    def _():
        for chunk in range(CHUNKS):
            own_one(chunk).wait_send()

    @pl.when(has_next)
    def _():
        for chunk in range(CHUNKS):
            own_two(chunk).wait_send()

    @pl.when(relays & has_one)
    def _():
        for chunk in range(CHUNKS):
            relay_on(chunk).wait_send()

    @pl.when(relays & has_next)
    def _():
        for chunk in range(CHUNKS):
            relay_two(chunk).wait_send()


def solution(mesh):
    servers = mesh.shape["srv"]
    blocks = mesh.shape["blk"]
    placed = (
        P("srv", "blk", "rep", None),
        P("srv", "blk", "rep"),
        P("srv", "blk", "rep"),
        P("srv", "blk", "rep"),
        P("srv", "blk", "rep"),
        P("srv", "rep"),
    )

    def on_device(queries, destination, offsets, key_rows, value_rows, lengths):
        block_rows, kv_width = key_rows.shape[1:]
        slot_rows = ROUNDS * R
        packed = (servers, KVH, QH // KVH * slot_rows, HD)
        window = (BACK + 1) * block_rows
        smem = pl.BlockSpec(memory_space=pltpu.SMEM)
        anywhere = pl.BlockSpec(memory_space=pl.ANY)
        dma = pltpu.SemaphoreType.DMA

        def body(*refs):
            kernel(servers, blocks, *refs)

        return pl.pallas_call(
            body,
            name="routed_attention",
            out_shape=pltpu.VMEM(queries.shape, queries.dtype),
            in_specs=[smem] * 3 + [anywhere] * 3,
            out_specs=pl.BlockSpec(memory_space=pltpu.VMEM),
            scratch_shapes=[
                pltpu.VMEM(queries.shape[2:], jnp.bfloat16),
                pltpu.VMEM((window, kv_width), jnp.bfloat16),
                pltpu.VMEM((window, kv_width), jnp.bfloat16),
                pltpu.VMEM(packed, jnp.bfloat16),
                pltpu.VMEM(packed, jnp.bfloat16),
                pltpu.VMEM((servers, slot_rows, LANES), jnp.int32),
                pltpu.VMEM((servers, slot_rows, LANES), jnp.int32),
                pltpu.VMEM(packed[:3] + (window,), jnp.float32),
                pltpu.VMEM(packed[:3] + (window,), jnp.bfloat16),
                pltpu.VMEM(packed, jnp.float32),
                pltpu.VMEM((KVH, queries.shape[2], QH // KVH * HD), jnp.float32),
                pltpu.VMEM(packed, jnp.bfloat16),
                pltpu.VMEM(packed, jnp.bfloat16),
                dma((3,)),
                dma((2, CHUNKS)),
                dma((2, CHUNKS)),
                dma((BACK, CHUNKS)),
                dma((servers,)),
                dma((servers,)),
                dma((servers,)),
                dma((servers,)),
                dma((servers, KVH)),
                dma((servers, KVH)),
            ],
            compiler_params=pltpu.CompilerParams(collective_id=0, has_side_effects=True),
        )(destination, offsets, lengths, queries, key_rows, value_rows)

    return jax.shard_map(
        on_device,
        mesh=mesh,
        in_specs=placed,
        out_specs=P("srv", "blk", "rep", None),
        check_vma=False,
    )
```

```python
import math

import jax
import jax.numpy as jnp
from jax import lax
from jax.experimental import pallas as pl
from jax.experimental.pallas import tpu as pltpu
from jax.sharding import PartitionSpec as P

QH = 32
KVH = 2
HD = 128
R = 4
ROUNDS = 2
BACK = 3
CHUNKS = 4
LANES = 128
MESH = pl.DeviceIdType.MESH


def each(count, body):
    if count <= 2:
        for index in range(count):
            body(index)
    else:
        lax.fori_loop(0, count, lambda index, carry: (body(index), carry)[1], 0)


def kernel(
    servers,
    blocks,
    destination,
    offsets,
    lengths,
    queries,
    key_rows,
    value_rows,
    out,
    own_queries,
    keys,
    values,
    query_out,
    query_in,
    place_out,
    place_in,
    scores,
    weights,
    totals,
    gathered,
    answers,
    returned,
    load_sem,
    own_send,
    relay_send,
    kv_recv,
    query_send,
    query_recv,
    place_send,
    place_recv,
    back_send,
    back_recv,
):
    me = lax.axis_index("srv")
    blk = lax.axis_index("blk")
    block_rows = key_rows.shape[1]
    tasks = destination.shape[2]
    per_round = tasks // ROUNDS
    groups = QH // KVH
    slot_rows = ROUNDS * R
    head_rows = groups * slot_rows
    scaling = 1.0 / math.sqrt(HD)
    docs = lengths.shape[1]

    load_queries = pltpu.make_async_copy(queries.at[0, 0], own_queries, load_sem.at[0])
    load_keys = pltpu.make_async_copy(
        key_rows.at[0], keys.at[pl.ds(0, block_rows)], load_sem.at[1]
    )
    load_values = pltpu.make_async_copy(
        value_rows.at[0], values.at[pl.ds(0, block_rows)], load_sem.at[2]
    )
    load_queries.start()
    load_keys.start()
    load_values.start()

    barrier = pltpu.get_barrier_semaphore()
    for hop in range(1, BACK):

        @pl.when(blk + hop < blocks)
        def _():
            pl.semaphore_signal(
                barrier, inc=1, device_id={"blk": blk + hop}, device_id_type=MESH
            )

        @pl.when(blk >= hop)
        def _():
            pl.semaphore_signal(
                barrier, inc=1, device_id={"blk": blk - hop}, device_id_type=MESH
            )

    def greet(step):
        peer = lax.rem(me + 1 + step, servers)
        pl.semaphore_signal(barrier, inc=1, device_id={"srv": peer}, device_id_type=MESH)

    each(servers - 1, greet)

    for hop in range(1, BACK + 1):

        @pl.when(blk < hop)
        def _():
            empty = jnp.zeros((block_rows, keys.shape[1]), keys.dtype)
            keys[pl.ds(hop * block_rows, block_rows), :] = empty
            values[pl.ds(hop * block_rows, block_rows), :] = empty

    load_queries.wait()
    all_rows = own_queries[...]
    row = lax.broadcasted_iota(jnp.int32, (slot_rows, tasks * R), 0)
    column = lax.broadcasted_iota(jnp.int32, (slot_rows, tasks * R), 1)
    column_target = jnp.full((slot_rows, tasks * R), -1, jnp.int32)
    for task in range(tasks):
        column_target = jnp.where(
            column // R == task, destination[0, 0, task], column_target
        )
    same_place = (row // R == column // (per_round * R)) & (row % R == column % R)
    place_row = lax.broadcasted_iota(jnp.int32, (slot_rows, LANES), 0)

    def pack(slot):
        chosen = jnp.where(same_place & (column_target == slot), 1.0, 0.0).astype(jnp.bfloat16)
        routed = jnp.dot(chosen, all_rows, preferred_element_type=jnp.float32)
        for g in range(KVH):
            parts = [
                routed[:, (g * groups + h) * HD : (g * groups + h + 1) * HD]
                for h in range(groups)
            ]
            query_out[slot, g] = jnp.concatenate(parts, axis=0).astype(jnp.bfloat16)
        start = jnp.zeros((slot_rows, LANES), jnp.int32)
        for turn in range(ROUNDS):
            offset = jnp.int32(0)
            for t in range(per_round):
                task = turn * per_round + t
                offset = jnp.where(
                    destination[0, 0, task] == slot, offsets[0, 0, task], offset
                )
            start = jnp.where(place_row // R == turn, offset, start)
        place_out[slot] = start + place_row % R + blk * block_rows

    each(servers, pack)

    neighbours = (
        jnp.minimum(blk, BACK - 1)
        + jnp.minimum(blocks - 1 - blk, BACK - 1)
        + (servers - 1)
    )
    pl.semaphore_wait(barrier, neighbours)

    def query_copy(slot, source):
        return pltpu.make_async_remote_copy(
            src_ref=query_out.at[slot],
            dst_ref=query_in.at[source],
            send_sem=query_send.at[slot],
            recv_sem=query_recv.at[source],
            device_id={"srv": slot},
            device_id_type=MESH,
        )

    def place_copy(slot, source):
        return pltpu.make_async_remote_copy(
            src_ref=place_out.at[slot],
            dst_ref=place_in.at[source],
            send_sem=place_send.at[slot],
            recv_sem=place_recv.at[source],
            device_id={"srv": slot},
            device_id_type=MESH,
        )

    def back_copy(slot, g, server):
        return pltpu.make_async_remote_copy(
            src_ref=answers.at[slot, g],
            dst_ref=returned.at[server, g],
            send_sem=back_send.at[slot, g],
            recv_sem=back_recv.at[server, g],
            device_id={"srv": slot},
            device_id_type=MESH,
        )

    pieces = CHUNKS // 2
    part_rows = block_rows // pieces

    def kv_copy(source, target, slot, hop, chunk, sent):
        part = chunk % pieces * part_rows
        low = hop * block_rows + part
        return pltpu.make_async_remote_copy(
            src_ref=source[chunk // pieces].at[pl.ds(slot * block_rows + part, part_rows)],
            dst_ref=(keys, values)[chunk // pieces].at[pl.ds(low, part_rows)],
            send_sem=sent.at[chunk],
            recv_sem=kv_recv.at[hop - 1, chunk],
            device_id={"blk": target},
            device_id_type=MESH,
        )

    own = (key_rows.at[0], value_rows.at[0])
    held = (keys, values)
    is_odd = lax.rem(blk, 2) == 1
    relays = (blk >= 2) & jnp.logical_not(is_odd)
    late = is_odd & (lax.axis_index("rep") == 1)
    has_one = blk + 1 < blocks
    has_next = blk + 2 < blocks

    def own_one(chunk):
        return kv_copy(own, blk + 1, 0, 1, chunk, own_send.at[0])

    def own_two(chunk):
        return kv_copy(own, blk + 2, 0, 2, chunk, own_send.at[1])

    def relay_on(chunk):
        return kv_copy(held, blk + 1, 2, 3, chunk, relay_send.at[0])

    def arrived(hop, chunk):
        return kv_copy(held, blk, 0, hop, chunk, own_send.at[0])

    def relay_two(chunk):
        return kv_copy(held, blk + 2, 1, 3, chunk, relay_send.at[1])

    def await_all(hop, chunks):
        for chunk in chunks:
            arrived(hop, chunk).wait_recv()

    def take_two(chunk):
        arrived(2, chunk).wait_recv()

        @pl.when(has_one)
        def _():
            relay_on(chunk).start()

    def take_one(chunk):
        arrived(1, chunk).wait_recv()

        @pl.when(has_next)
        def _():
            relay_two(chunk).start()

    def send_queries(step):
        peer = lax.rem(me + 1 + step, servers)
        query_copy(peer, me).start()
        place_copy(peer, me).start()

    each(servers - 1, send_queries)
    @pl.when(has_one)
    def _():
        for chunk in range(CHUNKS):
            own_one(chunk).start()

    @pl.when(has_next & jnp.logical_not(late))
    def _():
        for chunk in range(CHUNKS):
            own_two(chunk).start()

    query_in[me] = query_out[me]
    place_in[me] = place_out[me]
    load_keys.wait()

    def score(slot, hop):
        for g in range(KVH):
            block = keys[pl.ds(hop * block_rows, block_rows), g * HD : (g + 1) * HD]
            scores[slot, g, :, hop * block_rows : (hop + 1) * block_rows] = lax.dot_general(
                query_in[slot, g],
                block,
                (((1,), (1,)), ((), ())),
                preferred_element_type=jnp.float32,
            )

    score(me, 0)
    first_half, second_half = range(pieces), range(pieces, CHUNKS)

    @pl.when(is_odd)
    def _():
        await_all(1, first_half)

    @pl.when(late)
    def _():
        await_all(1, second_half)

    @pl.when(has_next & late)
    def _():
        for chunk in range(CHUNKS):
            own_two(chunk).start()

    @pl.when(relays)
    def _():
        for chunk in range(CHUNKS):
            take_one(chunk)
            take_two(chunk)

    def first_scores(step):
        peer = lax.rem(me + 1 + step, servers)
        query_copy(peer, peer).wait_recv()
        place_copy(peer, peer).wait_recv()
        score(peer, 0)

    each(servers - 1, first_scores)
    each(servers, lambda slot: score(slot, 1))

    @pl.when(is_odd & (blk >= 2))
    def _():
        await_all(2, first_half)

    each(servers, lambda slot: score(slot, 2))

    @pl.when(blk >= 3)
    def _():
        await_all(3, first_half)

    each(servers, lambda slot: score(slot, 3))

    ends = []
    running = jnp.int32(0)
    for doc in range(docs):
        running = running + lengths[0, doc]
        ends.append(running)
    lane = lax.broadcasted_iota(jnp.int32, (slot_rows, LANES), 1)

    def weigh(slot):
        place = place_in[slot]
        first = jnp.zeros_like(place)
        for end in ends:
            first = jnp.where(end <= place, end, first)
        for g in range(KVH):
            logits = []
            highest = None
            for low in range(0, (BACK + 1) * block_rows, LANES):
                hop = low // block_rows
                at = (blk - hop) * block_rows + low % block_rows + lane
                allowed = (at <= place) & (at >= first)
                piece = scores[slot, g, :, low : low + LANES] * scaling
                piece = piece.reshape(groups, slot_rows, LANES)
                piece = jnp.where(allowed[None], piece, -1e30)
                logits.append(piece)
                highest = piece if highest is None else jnp.maximum(highest, piece)
            highest = jnp.max(highest, axis=2, keepdims=True)
            total = None
            for index, piece in enumerate(logits):
                weight = jnp.exp(piece - highest)
                total = weight if total is None else total + weight
                weights[slot, g, :, index * LANES : (index + 1) * LANES] = weight.reshape(
                    head_rows, LANES
                ).astype(jnp.bfloat16)
            total = jnp.sum(total, axis=2, keepdims=True).reshape(head_rows, 1)
            totals[slot, g] = jnp.broadcast_to(total, (head_rows, HD))

    def attend(slot, g):
        weighted = jnp.dot(
            weights[slot, g],
            values[:, g * HD : (g + 1) * HD],
            preferred_element_type=jnp.float32,
        )
        return (weighted / totals[slot, g]).astype(jnp.bfloat16)

    each(servers, weigh)
    load_values.wait()

    @pl.when(is_odd & jnp.logical_not(late))
    def _():
        await_all(1, second_half)

    @pl.when(is_odd & (blk >= 2))
    def _():
        await_all(2, second_half)

    @pl.when(blk >= 3)
    def _():
        await_all(3, second_half)

    def serve(step):
        peer = lax.rem(me + 1 + step, servers)
        for g in range(KVH):
            answers[peer, g] = attend(peer, g)
            back_copy(peer, g, me).start()

    each(servers - 1, serve)
    for g in range(KVH):
        returned[me, g] = attend(me, g)

    out_row = lax.broadcasted_iota(jnp.int32, (tasks * R, slot_rows), 0)
    from_row = lax.broadcasted_iota(jnp.int32, (tasks * R, slot_rows), 1)
    row_target = jnp.full((tasks * R, slot_rows), -1, jnp.int32)
    for task in range(tasks):
        row_target = jnp.where(out_row // R == task, destination[0, 0, task], row_target)
    aligned = (from_row // R == out_row // (per_round * R)) & (from_row % R == out_row % R)

    def unpack(slot, g):
        taken = jnp.where(aligned & (row_target == slot), 1.0, 0.0).astype(jnp.bfloat16)
        got = returned[slot, g].astype(jnp.float32)
        wide = [got[h * slot_rows : (h + 1) * slot_rows] for h in range(groups)]
        wide = jnp.concatenate(wide, axis=1).astype(jnp.bfloat16)
        return jnp.dot(taken, wide, preferred_element_type=jnp.float32)

    for g in range(KVH):
        gathered[g] = unpack(me, g)

    def collect(step):
        peer = lax.rem(me + 1 + step, servers)
        for g in range(KVH):
            back_copy(peer, g, peer).wait_recv()
            gathered[g] += unpack(peer, g)

    each(servers - 1, collect)
    for g in range(KVH):
        out[0, 0, :, g * groups * HD : (g + 1) * groups * HD] = gathered[g].astype(jnp.bfloat16)

    def finish(step):
        peer = lax.rem(me + 1 + step, servers)
        query_copy(peer, me).wait_send()
        place_copy(peer, me).wait_send()
        for g in range(KVH):
            back_copy(peer, g, me).wait_send()

    each(servers - 1, finish)
    @pl.when(has_one)
    def _():
        for chunk in range(CHUNKS):
            own_one(chunk).wait_send()

    @pl.when(has_next)
    def _():
        for chunk in range(CHUNKS):
            own_two(chunk).wait_send()

    @pl.when(relays & has_one)
    def _():
        for chunk in range(CHUNKS):
            relay_on(chunk).wait_send()

    @pl.when(relays & has_next)
    def _():
        for chunk in range(CHUNKS):
            relay_two(chunk).wait_send()


def solution(mesh):
    servers = mesh.shape["srv"]
    blocks = mesh.shape["blk"]
    placed = (
        P("srv", "blk", "rep", None),
        P("srv", "blk", "rep"),
        P("srv", "blk", "rep"),
        P("srv", "blk", "rep"),
        P("srv", "blk", "rep"),
        P("srv", "rep"),
    )

    def on_device(queries, destination, offsets, key_rows, value_rows, lengths):
        block_rows, kv_width = key_rows.shape[1:]
        slot_rows = ROUNDS * R
        packed = (servers, KVH, QH // KVH * slot_rows, HD)
        window = (BACK + 1) * block_rows
        smem = pl.BlockSpec(memory_space=pltpu.SMEM)
        anywhere = pl.BlockSpec(memory_space=pl.ANY)
        dma = pltpu.SemaphoreType.DMA

        def body(*refs):
            kernel(servers, blocks, *refs)

        return pl.pallas_call(
            body,
            name="routed_attention",
            out_shape=pltpu.VMEM(queries.shape, queries.dtype),
            in_specs=[smem] * 3 + [anywhere] * 3,
            out_specs=pl.BlockSpec(memory_space=pltpu.VMEM),
            scratch_shapes=[
                pltpu.VMEM(queries.shape[2:], jnp.bfloat16),
                pltpu.VMEM((window, kv_width), jnp.bfloat16),
                pltpu.VMEM((window, kv_width), jnp.bfloat16),
                pltpu.VMEM(packed, jnp.bfloat16),
                pltpu.VMEM(packed, jnp.bfloat16),
                pltpu.VMEM((servers, slot_rows, LANES), jnp.int32),
                pltpu.VMEM((servers, slot_rows, LANES), jnp.int32),
                pltpu.VMEM(packed[:3] + (window,), jnp.float32),
                pltpu.VMEM(packed[:3] + (window,), jnp.bfloat16),
                pltpu.VMEM(packed, jnp.float32),
                pltpu.VMEM((KVH, queries.shape[2], QH // KVH * HD), jnp.float32),
                pltpu.VMEM(packed, jnp.bfloat16),
                pltpu.VMEM(packed, jnp.bfloat16),
                dma((3,)),
                dma((2, CHUNKS)),
                dma((2, CHUNKS)),
                dma((BACK, CHUNKS)),
                dma((servers,)),
                dma((servers,)),
                dma((servers,)),
                dma((servers,)),
                dma((servers, KVH)),
                dma((servers, KVH)),
            ],
            compiler_params=pltpu.CompilerParams(collective_id=0, has_side_effects=True),
        )(destination, offsets, lengths, queries, key_rows, value_rows)

    return jax.shard_map(
        on_device,
        mesh=mesh,
        in_specs=placed,
        out_specs=P("srv", "blk", "rep", None),
        check_vma=False,
    )
```
